32 devices in a mesh: ctx: 16 (over z, y, x), fsdp: 2 (over core).
Axes of the slice: x: 2, y: 2, z: 4, core: 2. Of those that a mesh axis runs over, the one named last changes fastest.
Arguments:
- hidden_in: bfloat16 [2, 16, 2, 246, 768], P('fsdp', 'ctx'), may hold values from -6 to 6
- read_memory: bfloat16 [2, 16, 2, 10, 768], P('fsdp', 'ctx'), may hold values from -6 to 6
- doc_ids: int32 [2, 8192], P('fsdp'), may hold values from 0 to 63, never falling along the last dimension, each value on 1 to 1024 neighbouring positions
- cotangent: bfloat16 [2, 16, 2, 256, 768], P('fsdp', 'ctx'), may hold values from -6 to 6
- in_weight: bfloat16 [2, 768, 2304], P(None, 'fsdp'), may hold values from -0.21875 to 0.21875
- in_bias: bfloat16 [2, 1536], P(None, 'fsdp'), may hold values from -1.5 to 1.5
- out_weight: bfloat16 [2, 768, 768], P(None, 'fsdp'), may hold values from -0.875 to 0.875
- out_bias: bfloat16 [2, 768], P(None, 'fsdp'), may hold values from -1.5 to 1.5
- gain_one: bfloat16 [2, 768], P(None, 'fsdp'), may hold values from 0.5 to 1.5
- shift_one: bfloat16 [2, 768], P(None, 'fsdp'), may hold values from -1.5 to 1.5
- up_weight: bfloat16 [2, 768, 3072], P(None, 'fsdp'), may hold values from -0.21875 to 0.21875
- up_bias: bfloat16 [2, 3072], P(None, 'fsdp'), may hold values from -2.5 to 2.5
- down_weight: bfloat16 [2, 3072, 768], P(None, 'fsdp'), may hold values from -0.109375 to 0.109375
- down_bias: bfloat16 [2, 768], P(None, 'fsdp'), may hold values from -1.5 to 1.5
- gain_two: bfloat16 [2, 768], P(None, 'fsdp'), may hold values from 0.5 to 1.5
- shift_two: bfloat16 [2, 768], P(None, 'fsdp'), may hold values from -1.5 to 1.5
Outputs:
- activations: bfloat16 [2, 16, 2, 256, 768], P('fsdp', 'ctx')
- new_memory: bfloat16 [2, 16, 2, 10, 768], P('fsdp', 'ctx')
- input_grad: bfloat16 [2, 16, 2, 246, 768], P('fsdp', 'ctx')
- memory_grad: bfloat16 [2, 16, 2, 10, 768], P('fsdp', 'ctx')
- in_weight_grad: float32 [2, 768, 2304], P(None, 'fsdp')
- in_bias_grad: float32 [2, 1536], P(None, 'fsdp')
- out_weight_grad: float32 [2, 768, 768], P(None, 'fsdp')
- out_bias_grad: float32 [2, 768], P(None, 'fsdp')
- gain_one_grad: float32 [2, 768], P(None, 'fsdp')
- shift_one_grad: float32 [2, 768], P(None, 'fsdp')
- up_weight_grad: float32 [2, 768, 3072], P(None, 'fsdp')
- up_bias_grad: float32 [2, 3072], P(None, 'fsdp')
- down_weight_grad: float32 [2, 3072, 768], P(None, 'fsdp')
- down_bias_grad: float32 [2, 768], P(None, 'fsdp')
- gain_two_grad: float32 [2, 768], P(None, 'fsdp')
- shift_two_grad: float32 [2, 768], P(None, 'fsdp')
The draws below stay inside these ranges and needn't reach their ends.
Inputs may be any that keep to these rules, and one draw needn't show every extreme that they name: `doc_ids`: document numbers never fall along a sequence; each document holds 1 to min(1024, 2048) rows, one exactly that many.
All inputs are finite; a program needn't handle non-finite values.
Results may differ from the reference program's by a relative error of at most 0.024.
Values may be sent and summed in bfloat16 or wider, within the bound.
A program may use at most 320 MiB of HBM per device.

```python
import math
import jax
import jax.numpy as jnp
import numpy as np
from jax import lax

D = 768
HEADS = 12
HEAD_DIM = 64
FF = 3072
LAYERS = 2
MEM = 10
SEG = 256
INPUT_ROWS = 246
SEQLEN = 8192
SEQS = 2
N_CTX = 16


def levels(stream_key, extent, split, smallest, top_value):
    def one(axis_at, shards_of):
        draws = jax.random.uniform(jax.random.fold_in(jax.random.fold_in(stream_key, 6), axis_at), (shards_of,), jnp.float32, smallest / len(split), top_value / len(split))
        return jnp.repeat(jnp.exp(draws), extent[axis_at] // shards_of).reshape((-1,) + (1,) * (len(extent) - axis_at - 1))

    level = one(*split[0])
    for cut in split[1:]:
        level = level * one(*cut)
    return level


def length_profile(amount, total, bound, slope):
    loads = [(1 << 20) // math.isqrt(standing ** slope) + 1 for standing in range(2, amount + 1)]
    spare, counts = total - bound - (amount - 1), [1] * (amount - 1)
    while spare > 0:
        movable = [i for i in range(amount - 1) if counts[i] < bound]
        mass, remaining = sum([loads[i] for i in movable]), spare
        for i in movable:
            more = min(bound - counts[i], max(1, remaining * loads[i] // mass), spare)
            counts[i] = counts[i] + more
            spare = spare - more
    return np.array([bound] + counts)


def ragged_sizes(stream_key, count, total, bound, lean):
    if count == 2:
        one = jax.random.randint(stream_key, (), max(1, total - bound), min(bound, total - 1) + 1)
        return jnp.stack([one, total - one])
    lengths = jnp.asarray(length_profile(count, total, bound, lean), jnp.int32)
    couples = (count - 1) // 2
    donor, sink = lengths[1:1 + 2 * couples:2], lengths[2:2 + 2 * couples:2]
    margin = jnp.minimum(donor - 1, bound - sink)
    moved = jax.random.randint(jax.random.fold_in(stream_key, 1), (couples,), 0, 1 << 20) % (margin + 1)
    lengths = lengths.at[1:1 + 2 * couples:2].set(donor - moved).at[2:2 + 2 * couples:2].set(sink + moved)
    return lengths[jax.random.permutation(jax.random.fold_in(stream_key, 2), count)]


def normal_values(own_key, shape, deviation, reach, shards=(), held_as=jnp.bfloat16):
    loudness = levels(own_key, shape, shards, -0.22, 0.18) if shards else 1.0
    array = jax.random.normal(own_key, shape, jnp.float32) * deviation * loudness
    return jnp.minimum(jnp.maximum(array, -reach), reach).astype(held_as)


def setup_inputs(seed: int = 0) -> dict:
    splits = jax.random.split(jax.random.key(seed), 17)
    return {
        "hidden_in": normal_values(splits[0], (SEQS, N_CTX, 2, INPUT_ROWS, D), 1.0, 6.0, ((0, 2), (1, 16))),
        "read_memory": normal_values(splits[1], (SEQS, N_CTX, 2, MEM, D), 1.0, 6.0, ((0, 2), (1, 16))),
        "doc_ids": jax.vmap(lambda own: jnp.searchsorted(jnp.cumsum(ragged_sizes(own, SEQLEN // 128, SEQLEN, min(1024, SEQLEN // 4), 2)), jnp.arange(SEQLEN), side="right"))(jax.random.split(splits[2], SEQS)).reshape((SEQS, SEQLEN)).astype(jnp.int32),
        "cotangent": normal_values(splits[3], (SEQS, N_CTX, 2, SEG, D), 1.0, 6.0, ((0, 2), (1, 16))),
        "in_weight": normal_values(splits[4], (LAYERS, D, 3 * D), D ** -0.5, 0.21875, ((1, 2),)),
        "in_bias": normal_values(splits[5], (LAYERS, 2 * D), 0.3, 1.5, ((1, 2),)),
        "out_weight": normal_values(splits[6], (LAYERS, D, D), (D // 16) ** -0.5, 0.875, ((1, 2),)),
        "out_bias": normal_values(splits[7], (LAYERS, D), 0.3, 1.5, ((1, 2),)),
        "gain_one": jnp.clip(1.0 + 0.1 * jax.random.normal(splits[8], (LAYERS, D), jnp.float32), 0.5, 1.5).astype(jnp.bfloat16),
        "shift_one": normal_values(splits[9], (LAYERS, D), 0.3, 1.5, ((1, 2),)),
        "up_weight": normal_values(splits[10], (LAYERS, D, FF), D ** -0.5, 0.21875, ((1, 2),)),
        "up_bias": normal_values(splits[11], (LAYERS, FF), 0.5, 2.5, ((1, 2),)),
        "down_weight": normal_values(splits[12], (LAYERS, FF, D), FF ** -0.5, 0.109375, ((1, 2),)),
        "down_bias": normal_values(splits[13], (LAYERS, D), 0.3, 1.5, ((1, 2),)),
        "gain_two": jnp.clip(1.0 + 0.1 * jax.random.normal(splits[14], (LAYERS, D), jnp.float32), 0.5, 1.5).astype(jnp.bfloat16),
        "shift_two": normal_values(splits[15], (LAYERS, D), 0.3, 1.5, ((1, 2),)),
    }


@jax.custom_vjp
def low(v):
    return lax.optimization_barrier(v.astype(jnp.bfloat16)).astype(jnp.float32)

@jax.custom_vjp
def low_back(v):
    return v

def low_keep(v):
    return (low(v), None)

def low_pass(kept, grad):
    return (grad,)

def back_keep(v):
    return (v, None)

def back_low(kept, grad):
    return (low(grad),)
low.defvjp(low_keep, low_pass)
low_back.defvjp(back_keep, back_low)
EPSILON = 1e-06
NEGATIVE = -1e+30
HIGHEST_PRECISION = lax.Precision.HIGHEST
query_block = 512
inverse_root = 0.7071067811865476

def layer_norm(inputs, norm_gain, norm_shift):
    row_mean = lax.optimization_barrier(jnp.mean(inputs, axis=-1, keepdims=True))
    centred = inputs - row_mean
    spread = lax.optimization_barrier(jnp.mean(centred * centred, axis=-1, keepdims=True))
    return centred * lax.rsqrt(spread + EPSILON) * norm_gain + norm_shift

def gelu_exact(values):
    return 0.5 * values * (1.0 + lax.erf(values * inverse_root))

def undeal(blocks):
    return jnp.concatenate([blocks[:, 0], blocks[::-1, 1]], axis=0)

def deal_blocks(blocks):
    half_count = blocks.shape[0] // 2
    return jnp.stack([blocks[:half_count], blocks[half_count:][::-1]], axis=1)

def attention(queries, keys, values, positions, documents):
    total_rows = queries.shape[0]

    def one_block(members):
        query_rows, query_pos, query_doc = members
        scores = low_back(jnp.einsum('qhd,khd->hqk', query_rows, keys, precision=HIGHEST_PRECISION))
        visible = (documents[None, :] == query_doc[:, None]) & (positions[None, :] <= query_pos[:, None])
        scores = jnp.where(visible[None], scores, NEGATIVE)
        row_peak = lax.optimization_barrier(jnp.max(scores, axis=-1, keepdims=True))
        exponents = jnp.exp(scores - row_peak)
        weights_soft = exponents / lax.optimization_barrier(jnp.sum(exponents, axis=-1, keepdims=True))
        return jnp.einsum('hqk,khd->qhd', low(weights_soft), values, precision=HIGHEST_PRECISION)
    block_count = total_rows // query_block
    result = lax.map(jax.checkpoint(one_block), (queries.reshape(block_count, query_block, HEADS, HEAD_DIM), positions.reshape(block_count, query_block), documents.reshape(block_count, query_block)))
    return result.reshape(total_rows, HEADS * HEAD_DIM)

def encoder_layer(inputs, weights, positions, documents):
    in_weight, in_bias, out_weight, out_bias, gain_one, shift_one, up_weight, up_bias, down_weight, down_bias, gain_two, shift_two = weights
    zeros_mid = jnp.zeros((D,), jnp.float32)
    bias_all = jnp.concatenate([in_bias[:D], zeros_mid, in_bias[D:]])
    mixed_rows = low(low_back(jnp.dot(low(inputs), in_weight, precision=HIGHEST_PRECISION) + bias_all))
    queries = (mixed_rows[:, :D] * 0.125).reshape(-1, HEADS, HEAD_DIM)
    keys = mixed_rows[:, D:2 * D].reshape(-1, HEADS, HEAD_DIM)
    values = mixed_rows[:, 2 * D:].reshape(-1, HEADS, HEAD_DIM)
    attended = low(low_back(attention(queries, keys, values, positions, documents)))
    branch = low_back(jnp.dot(attended, out_weight, precision=HIGHEST_PRECISION) + out_bias)
    middle = layer_norm(inputs + branch, gain_one, shift_one)
    hidden = low_back(jnp.dot(low(middle), up_weight, precision=HIGHEST_PRECISION) + up_bias)
    active = low(gelu_exact(hidden))
    branch_two = low_back(jnp.dot(active, down_weight, precision=HIGHEST_PRECISION) + down_bias)
    return layer_norm(middle + branch_two, gain_two, shift_two)

def reference(hidden_in, read_memory, doc_ids, cotangent, in_weight, in_bias, out_weight, out_bias, gain_one, shift_one, up_weight, up_bias, down_weight, down_bias, gain_two, shift_two):
    params = tuple((piece.astype(jnp.float32) for piece in (in_weight, in_bias, out_weight, out_bias, gain_one, shift_one, up_weight, up_bias, down_weight, down_bias, gain_two, shift_two)))
    positions = jnp.arange(SEQLEN, dtype=jnp.int32)

    def forward(inputs, weights, documents):
        middle = encoder_layer(inputs, tuple((piece[0] for piece in weights)), positions, documents)
        return encoder_layer(middle, tuple((piece[1] for piece in weights)), positions, documents)

    def one_sequence(totals, members):
        hidden_seq, memory_seq, documents, cot_seq = members
        blocks = undeal(jnp.concatenate([memory_seq, hidden_seq], axis=2)).astype(jnp.float32)
        inputs = blocks.reshape(SEQLEN, D)
        output, pull_back = jax.vjp(lambda values, weights: forward(values, weights, documents), inputs, params)
        grad_inputs, grad_params = pull_back(undeal(cot_seq).astype(jnp.float32).reshape(SEQLEN, D))
        output_low = output.astype(jnp.bfloat16).reshape(2 * N_CTX, SEG, D)
        memory_nat = undeal(memory_seq)
        memory_next = jnp.concatenate([memory_nat[:1], output_low[:-1, SEG - MEM:]], axis=0)
        grad_blocks = grad_inputs.reshape(2 * N_CTX, SEG, D)
        grad_text = grad_blocks[:, MEM:].astype(jnp.bfloat16)
        grad_memory = jnp.concatenate([grad_blocks[1:, :MEM], jnp.zeros((1, MEM, D), jnp.float32)], axis=0).astype(jnp.bfloat16)
        totals = tuple((running + extra for running, extra in zip(totals, grad_params)))
        return (totals, (deal_blocks(output_low), deal_blocks(memory_next), deal_blocks(grad_text), deal_blocks(grad_memory)))
    zero_totals = tuple((jnp.zeros_like(piece) for piece in params))
    totals, results = lax.scan(one_sequence, zero_totals, (hidden_in, read_memory, doc_ids, cotangent))
    return (results[0], results[1], results[2], results[3], totals[0], totals[1], totals[2], totals[3], totals[4], totals[5], totals[6], totals[7], totals[8], totals[9], totals[10], totals[11])
```

```python
import functools

import jax
import jax.numpy as jnp
from jax import lax
from jax.experimental import pallas as pl
from jax.experimental.pallas import tpu as pltpu
from jax.sharding import PartitionSpec as P

MESH = pl.DeviceIdType.MESH
HEAD_DIM = 64
EPSILON = 1e-06
NEGATIVE = -1e30
DOC_MAX = 1024
inverse_root = 0.7071067811865476
inverse_tau = 0.3989422804014327
BF = jnp.bfloat16
F32 = jnp.float32
ANY = pl.BlockSpec(memory_space=pl.ANY)
WHOLE = pl.BlockSpec(memory_space=pltpu.VMEM)
VMEM_LIMIT = 58 << 20


def nn(a, b):
    return lax.dot_general(a, b, (((1,), (0,)), ((), ())), preferred_element_type=F32)


def nt(a, b):
    return lax.dot_general(a, b, (((1,), (1,)), ((), ())), preferred_element_type=F32)


def tn(a, b):
    return lax.dot_general(a, b, (((0,), (0,)), ((), ())), preferred_element_type=F32)


def full(shape):
    return pl.BlockSpec(shape, lambda j: (0,) * len(shape))


def shape_of(shape, dtype):
    return jax.ShapeDtypeStruct(shape, dtype)


def attn_fwd(a, w_in, bias, start_col, seg):
    rows, width = a.shape
    own = start_col.shape[0]
    back = rows - own
    quad = 4 * HEAD_DIM
    steps = width // quad
    blocks = own // seg

    def kernel(a_ref, wq, wk, wv, bq, bv, st_ref, q_ref, k_ref, v_ref, o_ref, l_ref):
        def project(i, carry):
            at = pl.ds(pl.multiple_of(i * seg, seg), seg)
            part = a_ref[at, :]
            k_ref[at, :] = nn(part, wk[...]).astype(BF)
            v_ref[at, :] = (nn(part, wv[...]) + bv[...]).astype(BF)
            return carry

        lax.fori_loop(0, rows // seg, project, 0)

        def project_q(i, carry):
            part = a_ref[pl.ds(pl.multiple_of(back + i * seg, seg), seg), :]
            got = (nn(part, wq[...]) + bq[...]).astype(BF)
            q_ref[pl.ds(pl.multiple_of(i * seg, seg), seg), :] = got * jnp.asarray(0.125, BF)
            return carry

        lax.fori_loop(0, blocks, project_q, 0)

        row = lax.broadcasted_iota(jnp.int32, (seg, seg), 0)
        col = lax.broadcasted_iota(jnp.int32, (seg, seg), 1)
        low = col <= row
        lane = lax.broadcasted_iota(jnp.int32, (seg, 2 * HEAD_DIM), 1)
        mid = back - seg
        col_mid = lax.broadcasted_iota(jnp.int32, (seg, mid), 1)

        def one_block(i, carry):
            base = pl.multiple_of(i * seg, seg)
            at = pl.ds(base, seg)
            st = st_ref[at, :] - base
            see_edge = jnp.where(low, col + back, col) >= st
            see_mid = (col_mid + seg) >= st
            logs = jnp.zeros((seg, 2 * HEAD_DIM), F32)
            for pair in range(2):
                lanes = slice(pair * 2 * HEAD_DIM, (pair + 1) * 2 * HEAD_DIM)
                qp = q_ref[at, lanes]
                k_far = k_ref[at, lanes]
                k_mid = k_ref[pl.ds(base + seg, mid), lanes]
                k_own = k_ref[pl.ds(base + back, seg), lanes]
                v_far = v_ref[at, lanes]
                v_mid = v_ref[pl.ds(base + seg, mid), lanes]
                v_own = v_ref[pl.ds(base + back, seg), lanes]
                outs = []
                for h in range(2):
                    mine = (lane >= HEAD_DIM) if h else (lane < HEAD_DIM)
                    qh = jnp.where(mine, qp, jnp.zeros_like(qp))
                    edge = jnp.where(low, nt(qh, k_own), nt(qh, k_far))
                    edge = jnp.where(see_edge, edge, NEGATIVE)
                    inner = jnp.where(see_mid, nt(qh, k_mid), NEGATIVE)
                    peak = jnp.maximum(
                        jnp.max(edge, axis=1, keepdims=True), jnp.max(inner, axis=1, keepdims=True)
                    )
                    edge = jnp.exp(edge - peak)
                    inner = jnp.exp(inner - peak)
                    total = jnp.sum(edge, axis=1, keepdims=True) + jnp.sum(inner, axis=1, keepdims=True)
                    got = nn(inner.astype(BF), v_mid)
                    got = got + nn(jnp.where(low, edge, 0.0).astype(BF), v_own)
                    got = got + nn(jnp.where(low, 0.0, edge).astype(BF), v_far)
                    outs.append(got / total)
                    logs = jnp.where(lane == 2 * pair + h, peak + jnp.log(total), logs)
                o_ref[at, lanes] = jnp.where(lane < HEAD_DIM, outs[0], outs[1]).astype(BF)
            l_ref[0, :, at] = logs.T[:8, :]
            return carry

        lax.fori_loop(0, blocks, one_block, 0)

    return pl.pallas_call(
        kernel,
        grid=(steps,),
        in_specs=[
            full((rows, width)),
            pl.BlockSpec((width, quad), lambda j: (0, j)),
            pl.BlockSpec((width, quad), lambda j: (0, steps + j)),
            pl.BlockSpec((width, quad), lambda j: (0, 2 * steps + j)),
            pl.BlockSpec((1, quad), lambda j: (0, j)),
            pl.BlockSpec((1, quad), lambda j: (0, steps + j)),
            full((own, 1)),
        ],
        out_specs=[
            pl.BlockSpec((own, quad), lambda j: (0, j)),
            pl.BlockSpec((rows, quad), lambda j: (0, j)),
            pl.BlockSpec((rows, quad), lambda j: (0, j)),
            pl.BlockSpec((own, quad), lambda j: (0, j)),
            pl.BlockSpec((1, 8, own), lambda j: (j, 0, 0)),
        ],
        out_shape=[
            shape_of((own, width), BF),
            shape_of((rows, width), BF),
            shape_of((rows, width), BF),
            shape_of((own, width), BF),
            shape_of((steps, 8, own), F32),
        ],
        compiler_params=pltpu.CompilerParams(vmem_limit_bytes=VMEM_LIMIT),
        name="attn_fwd",
    )(a, w_in, w_in, w_in, bias, bias, start_col)


def normalise(x):
    mean = jnp.mean(x, axis=-1, keepdims=True)
    centred = x - mean
    spread = jnp.mean(centred * centred, axis=-1, keepdims=True)
    scale = lax.rsqrt(spread + EPSILON)
    return centred * scale, scale


def ff_fwd(att, h, h_block, w_out, w_up, w_down, b_out, b_up, b_down, g1, s1, g2, s2):
    own, width = att.shape
    hidden = w_up.shape[1]
    chunk = 512
    steps = hidden // chunk

    def kernel(att_ref, h_ref, wo, wu, wd, bo, bu, bd, g1r, s1r, g2r, s2r,
               xh1, rs1, mid_low, act, gp, xh2, rs2, out, out_low, middle, acc):
        j = pl.program_id(0)

        @pl.when(j == 0)
        def _():
            x = h_ref[...].astype(F32) + (nn(att_ref[...], wo[...]) + bo[...])
            xh, sc = normalise(x)
            xh1[...] = xh
            rs1[...] = sc
            m = xh * g1r[...] + s1r[...]
            middle[...] = m
            mid_low[...] = m.astype(BF)
            acc[...] = jnp.zeros_like(acc)

        hid = nn(mid_low[...], wu[...]) + bu[...]
        scaled = hid * inverse_root
        half = 0.5 * (1.0 + lax.erf(scaled))
        low = (hid * half).astype(BF)
        act[...] = low
        gp[...] = (half + hid * (jnp.exp(-(scaled * scaled)) * inverse_tau)).astype(BF)
        acc[...] += nn(low, wd[...])

        @pl.when(j == steps - 1)
        def _():
            x = middle[...] + (acc[...] + bd[...])
            xh, sc = normalise(x)
            xh2[...] = xh
            rs2[...] = sc
            y = xh * g2r[...] + s2r[...]
            out[...] = y
            out_low[...] = y.astype(BF)

    row = full((1, width))
    return pl.pallas_call(
        kernel,
        grid=(steps,),
        in_specs=[
            full((own, width)),
            pl.BlockSpec((own, width), lambda j: (h_block, 0)),
            full((width, width)),
            pl.BlockSpec((width, chunk), lambda j: (0, j)),
            pl.BlockSpec((chunk, width), lambda j: (j, 0)),
            row,
            pl.BlockSpec((1, chunk), lambda j: (0, j)),
            row, row, row, row, row,
        ],
        out_specs=[
            full((own, width)),
            full((own, 1)),
            full((own, width)),
            pl.BlockSpec((own, chunk), lambda j: (0, j)),
            pl.BlockSpec((own, chunk), lambda j: (0, j)),
            full((own, width)),
            full((own, 1)),
            full((own, width)),
            full((own, width)),
        ],
        out_shape=[
            shape_of((own, width), F32),
            shape_of((own, 1), F32),
            shape_of((own, width), BF),
            shape_of((own, hidden), BF),
            shape_of((own, hidden), BF),
            shape_of((own, width), F32),
            shape_of((own, 1), F32),
            shape_of((own, width), F32),
            shape_of((own, width), BF),
        ],
        scratch_shapes=[pltpu.VMEM((own, width), F32), pltpu.VMEM((own, width), F32)],
        compiler_params=pltpu.CompilerParams(vmem_limit_bytes=VMEM_LIMIT),
        name="ff_fwd",
    )(att, h, w_out, w_up, w_down, b_out, b_up, b_down, g1, s1, g2, s2)


def norm_back(dy, xh, scale, gain):
    d = dy * gain
    mean_d = jnp.mean(d, axis=-1, keepdims=True)
    mean_dx = jnp.mean(d * xh, axis=-1, keepdims=True)
    return scale * (d - mean_d - xh * mean_dx)


def column_sum(x):
    return jnp.sum(x, axis=0, keepdims=True)


def ff_bwd(grads, xh2, rs2, g2, gp, act, w_down, w_up, mid_low, xh1, rs1, g1, w_out, att, pick):
    own, width = att.shape
    hidden = w_up.shape[1]
    chunk = width
    steps = hidden // chunk
    count = len(grads)
    groups = pick.shape[0]

    def kernel(*refs):
        g_refs = refs[:count]
        (xh2r, rs2r, g2r, gpr, actr, wd, wu, midr, xh1r, rs1r, g1r, wo, attr, pickr,
         dwd, dwu, dwo, small, dr1, do, delta, dr2, df, dm, mid_t) = refs[count:]
        j = pl.program_id(0)

        @pl.when(j == 0)
        def _():
            g = g_refs[0][...].astype(F32)
            for extra in g_refs[1:]:
                g = g + extra[...].astype(F32)
            xh = xh2r[...]
            small[...] = jnp.zeros_like(small)
            small[0:1, :] = column_sum(g * xh)
            small[1:2, :] = column_sum(g)
            d = norm_back(g, xh, rs2r[...], g2r[...])
            dr2[...] = d
            low = d.astype(BF)
            df[...] = low
            small[2:3, :] = column_sum(low.astype(F32))
            dm[...] = d
            mid_t[...] = midr[...].T

        dff = df[...]
        d_act = nt(dff, wd[...])
        dh = (d_act * gpr[...].astype(F32)).astype(BF)
        small[pl.ds(8 + j, 1), :] = column_sum(dh.astype(F32))
        dwd[...] = tn(actr[...], dff).astype(BF)
        dwu[...] = nn(mid_t[...], dh).astype(BF)
        dm[...] += nt(dh, wu[...])

        @pl.when(j == steps - 1)
        def _():
            g = dm[...]
            xh = xh1r[...]
            small[3:4, :] = column_sum(g * xh)
            small[4:5, :] = column_sum(g)
            d = norm_back(g, xh, rs1r[...], g1r[...])
            dr1[...] = d
            low = d.astype(BF)
            small[5:6, :] = column_sum(low.astype(F32))
            dwo[...] = tn(attr[...], low).astype(BF)
            back = nt(low, wo[...]).astype(BF)
            do[...] = back
            prod = back.astype(F32) * attr[...].astype(F32)
            high = prod.astype(BF)
            rest = (prod - high.astype(F32)).astype(BF)
            delta[...] = nt(pickr[...], high) + nt(pickr[...], rest)

    act_spec = pl.BlockSpec((own, chunk), lambda j: (0, j))
    return pl.pallas_call(
        kernel,
        grid=(steps,),
        in_specs=[full((own, width))] * count + [
            full((own, width)), full((own, 1)), full((1, width)),
            act_spec, act_spec,
            pl.BlockSpec((chunk, width), lambda j: (j, 0)),
            pl.BlockSpec((width, chunk), lambda j: (0, j)),
            full((own, width)), full((own, width)), full((own, 1)), full((1, width)),
            full((width, width)), full((own, width)), full((groups, width)),
        ],
        out_specs=[
            pl.BlockSpec((chunk, width), lambda j: (j, 0)),
            pl.BlockSpec((width, chunk), lambda j: (0, j)),
            full((width, width)),
            full((16, width)),
            full((own, width)),
            full((own, width)),
            full((groups, own)),
        ],
        out_shape=[
            shape_of((hidden, width), BF),
            shape_of((width, hidden), BF),
            shape_of((width, width), BF),
            shape_of((16, width), F32),
            shape_of((own, width), F32),
            shape_of((own, width), BF),
            shape_of((groups, own), F32),
        ],
        scratch_shapes=[
            pltpu.VMEM((own, width), F32),
            pltpu.VMEM((own, width), BF),
            pltpu.VMEM((own, width), F32),
            pltpu.VMEM((width, own), BF),
        ],
        compiler_params=pltpu.CompilerParams(vmem_limit_bytes=VMEM_LIMIT),
        name="ff_bwd",
    )(*grads, xh2, rs2, g2, gp, act, w_down, w_up, mid_low, xh1, rs1, g1, w_out, att, pick)


class Place:
    def __init__(self, contexts):
        self.n = contexts
        self.me = lax.axis_index("ctx")
        self.f = lax.axis_index("fsdp")
        self.odd = self.f % 2
        self.x = self.me % 2
        pair = self.me // 2
        self.is_low = self.x == self.odd
        self.chunk = jnp.where(self.is_low, pair, contexts - 1 - pair)
        self.half = jnp.where(self.is_low, 0, 1)
        self.mate = self.me + 1 - 2 * self.x

    def ctx_of(self, chunk):
        c = (chunk + self.n) % self.n
        return jnp.where(c < self.n // 2, 2 * c + self.odd, 2 * (self.n - 1 - c) + 1 - self.odd)


def greet(devices, count):
    barrier = pltpu.get_barrier_semaphore()
    for device in devices:
        pl.semaphore_signal(barrier, inc=1, device_id=device, device_id_type=MESH)
    pl.semaphore_wait(barrier, count)


def remote(src, dst, send, recv, device):
    return pltpu.make_async_remote_copy(
        src_ref=src, dst_ref=dst, send_sem=send, recv_sem=recv, device_id=device, device_id_type=MESH
    )


def gather_copies(shards, outs, bounce, peers, place, sems, loc):
    far, inward, outward = [], [], []
    for i, (src, dst) in enumerate(zip(shards, outs)):
        size = src.shape[0]
        here = dst.at[pl.ds(pl.multiple_of(place.f * size, 8), size)]
        for d, peer in enumerate(peers):
            far.append(remote(src, here, sems.at[0, i, d], sems.at[1, i, d], peer))
        inward.append(pltpu.make_async_copy(src, bounce[i], loc.at[0, i]))
        outward.append(pltpu.make_async_copy(bounce[i], here, loc.at[1, i]))
    return far, inward, outward


def fetch_window(x0, weights, small, contexts, fsdps, layer):
    seg, width = x0.shape[1:]
    own = 2 * seg
    rows = 3 * own
    count = len(weights)

    def kernel(*refs):
        x_ref, w_refs, small_ref = refs[0], refs[1:1 + count], refs[1 + count]
        win, w_outs, small_out = refs[2 + count], refs[3 + count:3 + 2 * count], refs[3 + 2 * count]
        send, recv, w_sem, w_loc, s_sem, loc = refs[4 + 2 * count:10 + 2 * count]
        bounce = refs[10 + 2 * count:]
        p = Place(contexts)
        peers = [(p.me, (p.f + d) % fsdps) for d in range(1, fsdps)]
        mate = (p.mate, p.f)
        ahead = [(p.ctx_of(p.chunk + s), p.f) for s in (1, 2)]
        behind = [(p.ctx_of(p.chunk - s), p.f) for s in (1, 2)]
        greet([mate] + behind + peers, 3 + fsdps - 1)
        slot = p.odd
        other = 1 - slot
        mine = x_ref.at[p.half]

        def at(start, s):
            return win.at[pl.ds(pl.multiple_of(start + s * seg, seg), seg)]

        swap = remote(x_ref.at[1 - p.half], at(2 * own, other), send.at[0], recv.at[0], mate)
        swap.start()
        keep = pltpu.make_async_copy(mine, at(2 * own, slot), loc.at[0])
        keep.start()
        first = [
            remote(mine, at((2 - s) * own, slot), send.at[s], recv.at[s], ahead[s - 1]) for s in (1, 2)
        ]
        for copy in first:
            copy.start()
        gathers, inward, outward = gather_copies(
            [r.at[layer] for r in w_refs], w_outs, bounce, peers, p, w_sem, w_loc
        )
        for i, peer in enumerate(peers):
            gathers.append(remote(small_ref, small_out.at[p.f], s_sem.at[0, i], s_sem.at[1, i], peer))
        gathers.append(pltpu.make_async_copy(small_ref, small_out.at[p.f], loc.at[1]))
        for copy in gathers + inward:
            copy.start()
        for copy, follow in zip(inward, outward):
            copy.wait()
            follow.start()
        swap.wait_recv()
        second = [
            remote(at(2 * own, other), at((2 - s) * own, other), send.at[2 + s], recv.at[2 + s], ahead[s - 1])
            for s in (1, 2)
        ]
        for copy in second:
            copy.start()
        keep.wait()
        for copy in gathers + outward + first + second:
            copy.wait()
        swap.wait_send()

    full_weights = [
        shape_of((w.shape[1] * fsdps,) + w.shape[2:], w.dtype) for w in weights
    ]
    return pl.pallas_call(
        kernel,
        out_shape=[shape_of((rows, width), BF)] + full_weights
        + [shape_of((fsdps,) + small.shape, small.dtype)],
        in_specs=[WHOLE] + [ANY] * count + [WHOLE],
        out_specs=[ANY] * (2 + count),
        scratch_shapes=[
            pltpu.SemaphoreType.DMA((5,)),
            pltpu.SemaphoreType.DMA((5,)),
            pltpu.SemaphoreType.DMA((2, count, max(1, fsdps - 1))),
            pltpu.SemaphoreType.DMA((2, count)),
            pltpu.SemaphoreType.DMA((2, max(1, fsdps - 1))),
            pltpu.SemaphoreType.DMA((2,)),
        ] + [pltpu.VMEM(w.shape[1:], w.dtype) for w in weights],
        compiler_params=pltpu.CompilerParams(
            collective_id=0, has_side_effects=True, vmem_limit_bytes=VMEM_LIMIT
        ),
        name="fetch_window",
    )(x0, *weights, small)


def share_window(low, weights, cot, contexts, fsdps, layer):
    own, width = low.shape
    seg = own // 2
    rows = 3 * own
    count = len(weights)

    def kernel(*refs):
        x_ref, w_refs, cot_ref = refs[0], refs[1:1 + count], refs[1 + count]
        win, w_outs, cot_out = refs[2 + count], refs[3 + count:3 + 2 * count], refs[3 + 2 * count]
        send, recv, w_sem, w_loc, loc = refs[4 + 2 * count:9 + 2 * count]
        bounce = refs[9 + 2 * count:]
        p = Place(contexts)
        peers = [(p.me, (p.f + d) % fsdps) for d in range(1, fsdps)]
        mate = (p.mate, p.f)
        ahead = [(p.ctx_of(p.chunk + s), p.f) for s in (1, 2)]
        behind = [(p.ctx_of(p.chunk - s), p.f) for s in (1, 2)]
        greet([mate] + behind + peers, 3 + fsdps - 1)
        slot = p.odd

        def part(s):
            return cot_out.at[pl.ds(pl.multiple_of(s * seg, seg), seg)]

        halo = [
            remote(x_ref, win.at[pl.ds((2 - s) * own, own)], send.at[s], recv.at[s], ahead[s - 1])
            for s in (1, 2)
        ]
        swap = remote(cot_ref.at[1 - p.half], part(1 - slot), send.at[0], recv.at[0], mate)
        keep = pltpu.make_async_copy(cot_ref.at[p.half], part(slot), loc.at[0])
        copy_own = pltpu.make_async_copy(x_ref, win.at[pl.ds(2 * own, own)], loc.at[1])
        copies = halo + [swap, keep, copy_own]
        far, inward, outward = gather_copies(
            [r.at[layer] for r in w_refs], w_outs, bounce, peers, p, w_sem, w_loc
        )
        for copy in copies + far + inward:
            copy.start()
        for copy, follow in zip(inward, outward):
            copy.wait()
            follow.start()
        for copy in copies + far + outward:
            copy.wait()

    full_weights = [
        shape_of((w.shape[1] * fsdps,) + w.shape[2:], w.dtype) for w in weights
    ]
    return pl.pallas_call(
        kernel,
        out_shape=[shape_of((rows, width), BF)] + full_weights + [shape_of((own, width), BF)],
        in_specs=[WHOLE] + [ANY] * count + [WHOLE],
        out_specs=[ANY] * (2 + count),
        scratch_shapes=[
            pltpu.SemaphoreType.DMA((3,)),
            pltpu.SemaphoreType.DMA((3,)),
            pltpu.SemaphoreType.DMA((2, count, max(1, fsdps - 1))),
            pltpu.SemaphoreType.DMA((2, count)),
            pltpu.SemaphoreType.DMA((2,)),
        ] + [pltpu.VMEM(w.shape[1:], w.dtype) for w in weights],
        compiler_params=pltpu.CompilerParams(
            collective_id=1, has_side_effects=True, vmem_limit_bytes=VMEM_LIMIT
        ),
        name="share_window",
    )(low, *weights, cot)


class Piece:
    def __init__(self, sums, u, r, ready=False):
        pattern = sums.ready_pattern if ready else sums.pattern
        self.k = 5 * u + r
        self.slot = self.k + sums.n if ready else self.k
        self.ready = ready
        self.deep = is_deep(pattern[r])
        same = [is_deep(kind) == self.deep for kind in pattern]
        self.i = u * sum(same) + sum(same[:r])
        x_first = pattern[r] in ("xyz", "zxy")
        b0, b1 = (sums.bx, sums.by) if x_first else (sums.by, sums.bx)
        self.p0, self.p1 = (sums.x, sums.y) if x_first else (sums.y, sums.x)
        rows = sums.rows
        size = rows // 4 if self.deep else rows // 2
        base = sums.m * (rows // 2) if self.deep else 0
        self.first = (base + b0 * size, size)
        self.given = (base + (1 - b0) * size, size)
        start = base + b0 * size
        self.second = (start + b1 * (size // 2), size // 2)
        self.given_1 = (start + (1 - b1) * (size // 2), size // 2)
        self.column = (0, rows) if self.deep else self.second
        start, size = self.column
        self.mine = (start + sums.m * (size // 2), size // 2)
        self.theirs = (start + (1 - sums.m) * (size // 2), size // 2)
        self.own = self.second if self.deep else self.mine


def is_deep(kind):
    return kind[0] == "z"


FLAT = ("xyz", "yxz", "xyz", "yxz", "zxy")
MIXED = ("xyz", "zyx", "yxz", "zyx", "xyz")


class Sums:
    height = 128

    def __init__(self, shard, count, contexts, fsdps, width, gather=True, early=None, late_round=0, ready=0, lag=4, pattern=MIXED,
                 ready_pattern=FLAT):
        if contexts != 16:
            raise ValueError("needs 16 contexts")
        self.valid = min(shard, self.height)
        self.n = count
        self.rows = self.height
        self.width = width
        self.fsdps = fsdps
        self.others = fsdps - 1
        self.stride = contexts // 4
        self.gather = gather
        self.early = count if early is None else early
        self.gap = 0 if early is None else max(0, late_round - self.early // 5)
        self.ready = ready
        self.pattern, self.ready_pattern = pattern, ready_pattern
        self.lag = lag
        self.stages = 9 if gather else 5
        last = max(count + 5 * self.gap + (self.stages - 1) * self.lag, ready + 4 * self.lag if ready else 0)
        self.rounds = -(-last // 5)

    def scratch(self):
        n, r, w = self.n, self.rows, self.width
        nd = max(1, self.others)
        n_c = sum(is_deep(self.pattern[k % 5]) for k in range(n))
        n_a = max(1, n - n_c)
        n_c = max(1, n_c)
        dma = pltpu.SemaphoreType.DMA
        both = n + self.ready
        return [
            pltpu.VMEM((n, r, w), BF),
            pltpu.VMEM((n, nd, self.valid, w), BF),
            pltpu.VMEM((n_a, r // 2, w), BF),
            pltpu.VMEM((n_a, r // 4, w), BF),
            pltpu.VMEM((n_a, r // 4, w), BF),
            pltpu.VMEM((n_a, r // 8, w), BF),
            pltpu.VMEM((n_c, r // 4, w), BF),
            pltpu.VMEM((n_c, r // 8, w), BF),
            pltpu.VMEM((n_c, r, w), BF),
            pltpu.VMEM((n_c, r // 2, w), BF),
            dma((n,)), dma((nd,)), dma((n, nd)),
            dma((4, 2)), dma((4, n)),
            dma((10, 2)), dma((5, both)), dma((both,)),
        ]

    def bind(self, refs, out, compact=None, ready_in=None, ready_out=None):
        self.acc, self.got_f = refs[0], refs[1]
        self.got_0, self.got_1 = (refs[2], refs[6]), (refs[3], refs[7])
        self.got_z, self.got_y = (refs[4], refs[8]), (refs[5], refs[9])
        self.s_loc, self.s_f, self.r_f, self.send, self.recv, self.g_send, self.g_recv, self.s_own = refs[10:18]
        self.out, self.compact, self.ready_in, self.ready_out = out, compact, ready_in, ready_out
        me, f = lax.axis_index("ctx"), lax.axis_index("fsdp")
        self.me, self.f = me, f
        self.bx, self.by, z = me % 2, me // 2 % 2, me // self.stride
        self.mid = (z == 1) | (z == 2)
        self.end = (z == 0) | (z == 3)
        self.m = jnp.where(z == 2, 1, 0)
        up, down = me + self.stride, me - self.stride
        self.x = (me + 1 - 2 * self.bx, f)
        self.y = (me + 2 - 4 * self.by, f)
        self.to_mid = (jnp.where(z == 0, up, down), f)
        self.other_mid = (jnp.where(z == 1, up, down), f)
        self.to_end = (jnp.where(z == 1, down, up), f)
        self.peers = [(me, (f + d) % self.fsdps) for d in range(1, self.fsdps)]
        if self.rows > self.valid:
            self.acc[:, self.valid:, :] = jnp.zeros((self.n, self.rows - self.valid, self.width), BF)

    def signal_neighbours(self, barrier):
        def tell(device):
            pl.semaphore_signal(barrier, inc=1, device_id=device, device_id_type=MESH)

        for device in self.peers + [self.x, self.y]:
            tell(device)

        @pl.when(self.end)
        def _():
            tell(self.to_mid)

        @pl.when(self.mid)
        def _():
            tell(self.other_mid)
            tell(self.to_end)

        return self.others + 2 + jnp.where(self.mid, 2, 1)

    def load(self, i, source):
        pltpu.make_async_copy(source(self.f), self.acc.at[i, pl.ds(0, self.valid)], self.s_loc.at[i]).start()
        for d, peer in enumerate(self.peers):
            remote(source(peer[1]), self.got_f.at[i, d], self.s_f.at[d], self.r_f.at[i, d], peer).start()

    def f_copy(self, k, d):
        ref = self.got_f.at[k, d]
        return remote(ref, ref, self.s_f.at[d], self.r_f.at[k, d], self.peers[d])

    def at(self, p, where):
        return self.acc.at[p.k, pl.ds(pl.multiple_of(where[0], 16), where[1])]

    def make(self, slot, p, src, dst, device):
        return remote(src, dst, self.send.at[slot, int(p.deep)], self.recv.at[slot, p.k], device)

    def copy_0(self, p):
        return self.make(0, p, self.at(p, p.given), self.got_0[p.deep].at[p.i], p.p0)

    def copy_1(self, p):
        return self.make(1, p, self.at(p, p.given_1), self.got_1[p.deep].at[p.i], p.p1)

    def copy_z(self, p):
        return self.make(2, p, self.at(p, p.column), self.got_z[p.deep].at[p.i], self.to_mid)

    def copy_y(self, p):
        return self.make(3, p, self.at(p, p.theirs), self.got_y[p.deep].at[p.i], self.other_mid)

    def add(self, p, where, part):
        rows = pl.ds(pl.multiple_of(where[0], 16), where[1])
        self.acc[p.k, rows, :] = self.acc[p.k, rows, :] + part[...]

    def take_f(self, p):
        mine = self.acc.at[p.k, pl.ds(0, self.valid)]
        pltpu.make_async_copy(mine, mine, self.s_loc.at[p.k]).wait()
        for d in range(self.others):
            self.f_copy(p.k, d).wait_recv()
        if self.others == 1:
            self.add(p, (0, self.valid), self.got_f.at[p.k, 0])
        else:
            value = mine[...].astype(F32)
            for d in range(self.others):
                value = value + self.got_f[p.k, d].astype(F32)
            mine[...] = value.astype(BF)

    def take_0(self, p):
        self.copy_0(p).wait_recv()
        self.add(p, p.first, self.got_0[p.deep].at[p.i])

    def take_1(self, p):
        self.copy_1(p).wait_recv()
        self.add(p, p.second, self.got_1[p.deep].at[p.i])

    def send_z(self, p):
        @pl.when(self.end)
        def _():
            self.copy_z(p).start()

    def take_z(self, p):
        @pl.when(self.mid)
        def _():
            self.copy_z(p).wait_recv()
            self.add(p, p.column, self.got_z[p.deep].at[p.i])
            self.copy_y(p).start()

    def take_y(self, p):
        self.copy_y(p).wait_recv()
        self.add(p, p.mine, self.got_y[p.deep].at[p.i])

    def place(self, p, where):
        ref = self.ready_out if p.ready else self.out
        return ref.at[p.k, pl.ds(pl.multiple_of(where[0], 16), where[1])]

    def held(self, p):
        return self.ready_in.at[p.k] if p.ready else self.at(p, p.own)

    def send_to(self, slot, p, where, device, held=False):
        spot = self.place(p, where)
        src = self.held(p) if held else spot
        sent = self.g_send.at[slot + 5 * p.ready, int(p.deep)]
        return remote(src, spot, sent, self.g_recv.at[slot, p.slot], device)

    def save(self, p):
        return pltpu.make_async_copy(self.held(p), self.place(p, p.own), self.s_own.at[p.slot])

    def gm(self, p):
        return self.send_to(0, p, p.mine, self.other_mid, held=not p.deep)

    def ge(self, p):
        return self.send_to(1, p, p.mine, self.to_end, held=not p.deep)

    def gf(self, p):
        return self.send_to(2, p, p.theirs, self.to_end)

    def g1(self, p):
        return self.send_to(3, p, p.second, p.p1, held=p.deep)

    def g0(self, p):
        return self.send_to(4, p, p.first, p.p0)

    def gather_stage(self, s, p):
        def on_mid(f):
            pl.when(self.mid)(f)

        def on_end(f):
            pl.when(self.end)(f)

        if not p.deep:
            if s == 0:
                @on_mid
                def _():
                    self.save(p).start()
                    self.gm(p).start()
                    self.ge(p).start()
            elif s == 1:
                @on_mid
                def _():
                    self.gm(p).wait_recv()
                    self.gf(p).start()
            elif s == 2:
                @on_mid
                def _():
                    self.save(p).wait()

                @on_end
                def _():
                    self.ge(p).wait_recv()
                    self.gf(p).wait_recv()

                self.g1(p).start()
            elif s == 3:
                self.g1(p).wait_recv()
                self.g0(p).start()
            else:
                self.g0(p).wait_recv()
            return
        if s == 4:
            @on_end
            def _():
                self.ge(p).wait_recv()
                self.gf(p).wait_recv()
            return

        @on_mid
        def _():
            if s == 0:
                self.save(p).start()
                self.g1(p).start()
            elif s == 1:
                self.save(p).wait()
                self.g1(p).wait_recv()
                self.g0(p).start()
            elif s == 2:
                self.g0(p).wait_recv()
                self.gm(p).start()
                self.ge(p).start()
            else:
                self.gm(p).wait_recv()
                self.gf(p).start()

    def scatter_stage(self, s, p):
        if s == 0:
            self.take_f(p)
            if p.deep:
                self.send_z(p)
            else:
                self.copy_0(p).start()
        elif not p.deep:
            if s == 1:
                self.take_0(p)
                self.copy_1(p).start()
            elif s == 2:
                self.take_1(p)
                self.send_z(p)
            elif s == 3:
                self.take_z(p)
            else:
                @pl.when(self.mid)
                def _():
                    self.take_y(p)
        elif s == 1:
            self.take_z(p)
        else:
            @pl.when(self.mid)
            def _():
                if s == 2:
                    self.take_y(p)
                    self.copy_0(p).start()
                elif s == 3:
                    self.take_0(p)
                    self.copy_1(p).start()
                else:
                    self.take_1(p)

        if s == 4 and not self.gather:
            @pl.when(self.mid)
            def _():
                self.compact[p.k] = self.at(p, p.own)[...]

    def round(self, t):
        for j in range(5):
            for s in reversed(range(self.stages)):
                q, r = divmod(j - s * self.lag, 5)
                u = t + q
                at = 5 * u + r
                if self.gap:
                    late = at >= self.early + 5 * self.gap
                    live = (at >= 0) & (late | (at < self.early)) & (at < self.n + 5 * self.gap)
                    u = jnp.where(late, u - self.gap, u)
                else:
                    live = (at >= 0) & (at < self.n)

                @pl.when(live)
                def _(s=s, u=u, r=r):
                    p = Piece(self, u, r)
                    if s < 5:
                        self.scatter_stage(s, p)
                    if s >= 4 and self.gather:
                        self.gather_stage(s - 4, p)

            for s in reversed(range(5 if self.ready else 0)):
                q, r = divmod(j - s * self.lag, 5)
                u = t + q
                at = 5 * u + r

                @pl.when((at >= 0) & (at < self.ready))
                def _(s=s, u=u, r=r):
                    self.gather_stage(s, Piece(self, u, r, True))

    def finish(self):
        def drained(sem, height, pattern, count, deep):
            pieces = sum(is_deep(pattern[k % 5]) == deep for k in range(count))
            while pieces:
                some = min(pieces, self.n * self.rows // height)
                whole, rest = divmod(some * height, self.rows)
                if whole:
                    ref = self.acc.at[pl.ds(0, whole)]
                    pltpu.make_async_copy(ref, ref, sem).wait()
                if rest:
                    ref = self.acc.at[0, pl.ds(0, rest)]
                    pltpu.make_async_copy(ref, ref, sem).wait()
                pieces -= some

        for d in range(self.others):
            ref = self.got_f.at[:, d]
            pltpu.make_async_copy(ref, ref, self.s_f.at[d]).wait()
        rows = self.rows
        for deep in (False, True):
            i = int(deep)
            size = rows // 4 if deep else rows // 2
            column = rows if deep else rows // 4
            for count, ready in ((self.n, False), (self.ready, True)):
                pattern = self.ready_pattern if ready else self.pattern
                across, along_end, along_mid = [], [], []
                if not ready:
                    across += [(self.send.at[0, i], size), (self.send.at[1, i], size // 2)]
                    along_end += [(self.send.at[2, i], column)]
                    along_mid += [(self.send.at[3, i], column // 2)]
                if ready or self.gather:
                    base = 5 * ready
                    across += [(self.g_send.at[base + 3, i], size // 2), (self.g_send.at[base + 4, i], size)]
                    along_mid += [(self.g_send.at[base + j, i], column // 2) for j in range(3)]

                def wait(copies, pattern=pattern, count=count, deep=deep):
                    for sem, height in copies:
                        drained(sem, height, pattern, count, deep)

                if deep:
                    along_mid = across + along_mid
                else:
                    wait(across)

                @pl.when(self.mid)
                def _(along_mid=along_mid, wait=wait):
                    wait(along_mid)

                if along_end:
                    @pl.when(self.end)
                    def _(along_end=along_end, wait=wait):
                        wait(along_end)


def piece_list(arrays, width, fsdps, height):
    shard = width // fsdps
    size = min(shard, height)
    found = []
    for i, shape in enumerate(arrays):
        r, c = shape[-2:]
        per = r // fsdps
        for at in range(shape[0]) if len(shape) == 3 else [None]:
            for lane in range(c // width):
                for sub in range(per // size):
                    found.append((i, at, per, sub * size, lane * width))
    return found


STRIDE, STRIDE_LAST = 2, 3


def attn_bwd(a, w_in, q, k, v, do, logs, delta, start_row, dr1, seg, contexts, fsdps, early, extra, ready=None):
    rows, width = a.shape
    own = q.shape[0]
    back = rows - own
    if rows != 2 * width:
        raise ValueError("window rows")
    pair_lanes = 2 * HEAD_DIM
    pairs = width // pair_lanes
    last = len(extra) > 1
    shard = width // fsdps
    pieces = piece_list([g.shape for g in early], width, fsdps, Sums.height)
    n_early = len(pieces)
    size = min(shard, Sums.height)
    n_late = 3 * (shard // size) + 1 if last else 0
    blocks = own // seg
    cut = 256
    t_back = blocks * pairs
    t_own = t_back + back // seg
    t_weight = t_own + own // seg
    t_rest = t_weight + width // cut
    n_ready = ready.shape[0] if last else 0
    stride = STRIDE_LAST if last else STRIDE
    late_round = max(t_rest // stride + 1, -(-n_early // 5))
    engine = Sums(
        shard, n_early + n_late, contexts, fsdps, width, gather=last, early=n_early if last else None,
        late_round=late_round, ready=n_ready, lag=4 if last else 6, pattern=MIXED if last else FLAT,
    )
    rounds = t_rest + max(engine.rounds - t_rest // stride, 9)
    n_x, n_e = len(extra), len(early)

    def kernel(*refs):
        (a_hbm, w_hbm, q_ref, k_ref, v_ref, do_ref, l_ref, d_ref, st_ref, dr1_hbm) = refs[:10]
        x_refs, e_refs = refs[10:10 + n_x], refs[10 + n_x:10 + n_x + n_e]
        rest = refs[10 + n_x + n_e:]
        if last:
            ready_in, out_sums, dealt, memory, ready_out = rest[:5]
            rest = rest[5:]
        else:
            out_sums, dealt, memory, g_own, one, two, dw_out, db_out = rest[:8]
            rest = rest[8:]
        (w_ref, dk, dv, dk_all, dv_all, dq_all, g_back, dw, send, recv, loc, m_send, m_recv) = rest[:13]
        rest = rest[13:]
        if last:
            g_own, one, two, sm, sm_low = rest[:5]
            rest = rest[5:]
            low_ref = one
        else:
            low_ref = x_refs[0]
        if last:
            engine.bind(rest, out_sums, ready_in=ready_in, ready_out=ready_out)
        else:
            engine.bind(rest, None, compact=out_sums)
        p = Place(contexts)
        mate = (p.mate, p.f)
        ahead = [(p.ctx_of(p.chunk + s), p.f) for s in (1, 2)]
        behind = [(p.ctx_of(p.chunk - s), p.f) for s in (1, 2)]
        slot = p.odd
        shift = -1 if last else 1

        def holder(block):
            b = (block + 2 * contexts) % (2 * contexts)
            return jnp.where(b < contexts, b, 2 * contexts - 1 - b), jnp.where(b < contexts, 0, 1)

        targets = [holder(2 * p.chunk + s + shift) for s in (0, 1)]
        sources = [
            p.ctx_of(((b - shift + 2 * contexts) % (2 * contexts)) // 2)
            for b in (p.me, 2 * contexts - 1 - p.me)
        ]

        barrier = pltpu.get_barrier_semaphore()
        for device in [mate] + ahead:
            pl.semaphore_signal(barrier, inc=1, device_id=device, device_id_type=MESH)
        for ctx in sources:
            @pl.when(ctx != p.me)
            def _(ctx=ctx):
                pl.semaphore_signal(barrier, inc=1, device_id=(ctx, p.f), device_id_type=MESH)
        count = 3 + engine.signal_neighbours(barrier)
        for ctx, _ in targets:
            count = count + jnp.where(ctx != p.me, 1, 0)
        pl.semaphore_wait(barrier, count)

        fetch_w = pltpu.make_async_copy(w_hbm, w_ref, loc.at[1])
        fetch_r = pltpu.make_async_copy(dr1_hbm, g_own, loc.at[4])
        fetch_w.start()
        fetch_r.start()
        for i, (e, at, per, sub, lane) in enumerate(pieces):
            def source(part, e=e, at=at, per=per, sub=sub, lane=lane):
                rows_at = pl.ds(pl.multiple_of(part * per + sub, 8), size)
                ref = e_refs[e] if at is None else e_refs[e].at[at]
                return ref.at[rows_at, pl.ds(lane, width)]

            engine.load(i, source)

        def block_rows(s):
            return pl.ds(pl.multiple_of(s * seg, seg), seg)

        def deal(start):
            there = remote(low_ref.at[block_rows(1 - slot)], dealt.at[p.half], send.at[0], recv.at[0], mate)
            here = pltpu.make_async_copy(low_ref.at[block_rows(slot)], dealt.at[p.half], loc.at[2])
            if start:
                there.start()
                here.start()
            else:
                there.wait()
                here.wait()

        def memory_copies(start):
            for s, (ctx, half) in enumerate(targets):
                first = s * seg + (seg - 16 if shift > 0 else 0)
                src, dst = low_ref.at[pl.ds(first, 16)], memory.at[half]
                away = remote(src, dst, m_send.at[s], m_recv.at[half], (ctx, p.f))

                @pl.when(ctx != p.me)
                def _(away=away):
                    if start:
                        away.start()
                    else:
                        away.wait_send()

                if start:
                    @pl.when(ctx == p.me)
                    def _(src=src, dst=dst, half=half):
                        pltpu.make_async_copy(src, dst, m_recv.at[half]).start()

            if not start:
                for half in range(2):
                    pltpu.make_async_copy(memory.at[half], memory.at[half], m_recv.at[half]).wait()

        if not last:
            deal(True)
            memory_copies(True)

        key = lax.broadcasted_iota(jnp.int32, (seg, seg), 0)
        qry = lax.broadcasted_iota(jnp.int32, (seg, seg), 1)
        low = key <= qry
        lane_id = lax.broadcasted_iota(jnp.int32, (seg, pair_lanes), 1)
        mid = back - seg
        key_mid = lax.broadcasted_iota(jnp.int32, (mid, seg), 0)

        def one_block(index):
            pair, i = index // blocks, index % blocks
            lanes = pl.ds(pl.multiple_of(pair * pair_lanes, pair_lanes), pair_lanes)

            @pl.when(i == 0)
            def _():
                dk[...] = jnp.zeros_like(dk)
                dv[...] = jnp.zeros_like(dv)

            base = pl.multiple_of(i * seg, seg)
            at = pl.ds(base, seg)
            st = st_ref[:, at] - base
            see_edge = jnp.where(low, key + back, key) >= st
            see_mid = (key_mid + seg) >= st
            far, near, inn = at, pl.ds(base + back, seg), pl.ds(base + seg, mid)
            qp, dop = q_ref[at, lanes], do_ref[at, lanes]
            k_far, k_mid, k_own = k_ref[far, lanes], k_ref[inn, lanes], k_ref[near, lanes]
            k_far_t, k_mid_t, k_own_t = k_far.T, k_mid.T, k_own.T
            v_far, v_mid, v_own = v_ref[far, lanes], v_ref[inn, lanes], v_ref[near, lanes]
            q2, do2, p_far, p_mid, p_own, s_far, s_mid, s_own, dqs = [], [], [], [], [], [], [], [], []
            for h in range(2):
                mine = (lane_id >= HEAD_DIM) if h else (lane_id < HEAD_DIM)
                qh = jnp.where(mine, qp, jnp.zeros_like(qp))
                doh = jnp.where(mine, dop, jnp.zeros_like(dop))
                stat = pair % 2 * 2 + h
                log_row = l_ref[pair // 2, pl.ds(stat, 1), at]
                del_row = d_ref[pair // 2, pl.ds(stat, 1), at]
                edge = jnp.where(low, nt(k_own, qh), nt(k_far, qh))
                edge = jnp.exp(jnp.where(see_edge, edge - log_row, NEGATIVE))
                inner = jnp.exp(jnp.where(see_mid, nt(k_mid, qh) - log_row, NEGATIVE))
                d_edge = edge * (jnp.where(low, nt(v_own, doh), nt(v_far, doh)) - del_row)
                d_inner = (inner * (nt(v_mid, doh) - del_row)).astype(BF)
                d_own = jnp.where(low, d_edge, 0.0).astype(BF)
                d_far = jnp.where(low, 0.0, d_edge).astype(BF)
                part = slice(h * HEAD_DIM, (h + 1) * HEAD_DIM)
                dqs.append(nn(k_mid_t[part], d_inner) + nn(k_own_t[part], d_own) + nn(k_far_t[part], d_far))
                q2.append(qh)
                do2.append(doh)
                p_far.append(jnp.where(low, 0.0, edge).astype(BF))
                p_own.append(jnp.where(low, edge, 0.0).astype(BF))
                p_mid.append(inner.astype(BF))
                s_far.append(d_far)
                s_own.append(d_own)
                s_mid.append(d_inner)
            q2 = jnp.concatenate(q2, axis=0)
            do2 = jnp.concatenate(do2, axis=0)
            dv[far, :] += nn(jnp.concatenate(p_far, axis=1), do2)
            dv[inn, :] += nn(jnp.concatenate(p_mid, axis=1), do2)
            dv[near, :] += nn(jnp.concatenate(p_own, axis=1), do2)
            dk[far, :] += nn(jnp.concatenate(s_far, axis=1), q2)
            dk[inn, :] += nn(jnp.concatenate(s_mid, axis=1), q2)
            dk[near, :] += nn(jnp.concatenate(s_own, axis=1), q2)
            dq_all[at, lanes] = (jnp.concatenate(dqs, axis=0).T * 0.125).astype(BF)

            @pl.when(i == blocks - 1)
            def _():
                dk_all[:, lanes] = dk[...].astype(BF)
                dv_all[:, lanes] = dv[...].astype(BF)

        bufs = (one, two)

        def back_rows(i):
            at = block_rows(i)
            got = nt(dk_all[at, :], w_ref[:, width:2 * width]) + nt(dv_all[at, :], w_ref[:, 2 * width:])
            g_back[at, :] = got.astype(BF)

        order = (1 - slot, slot)

        def halo_copies():
            found = []
            for i, s in enumerate(order):
                for j in (1, 2):
                    at = pl.multiple_of((2 - j) * own + s * seg, seg)
                    found.append(
                        remote(
                            g_back.at[pl.ds(at, seg)], bufs[j - 1].at[block_rows(s)],
                            send.at[2 * i + j], recv.at[2 * i + j], behind[j - 1],
                        )
                    )
            return found

        def own_rows(i):
            at = block_rows(i)
            there = pl.ds(pl.multiple_of(back + i * seg, seg), seg)
            got = nt(dk_all[there, :], w_ref[:, width:2 * width]) + nt(dv_all[there, :], w_ref[:, 2 * width:])
            g_own[at, :] += got + nt(dq_all[at, :], w_ref[:, :width])

        fetch_a = [
            pltpu.make_async_copy(
                a_hbm.at[pl.ds(i * width, width)], w_ref.at[:, pl.ds(i * width, width)], loc.at[i]
            )
            for i in range(2)
        ]

        def weight_rows(i):
            start = pl.multiple_of(i * cut, cut)
            at = pl.ds(start, cut)
            first = w_ref[:, at].T
            second = w_ref[:, pl.ds(pl.multiple_of(width + start, cut), cut)].T
            dw[0, at, :] = nn(second[:, back - width:], dq_all[...]).astype(BF)
            dw[1, at, :] = (nn(first, dk_all[:width, :]) + nn(second, dk_all[width:, :])).astype(BF)
            dw[2, at, :] = (nn(first, dv_all[:width, :]) + nn(second, dv_all[width:, :])).astype(BF)

        def late_pieces():
            for j in range(3):
                for sub in range(shard // size):
                    engine.load(
                        n_early + j * (shard // size) + sub,
                        lambda part, j=j, sub=sub: dw.at[j, pl.ds(pl.multiple_of(part * shard + sub * size, 16), size)],
                    )

            sm[...] = jnp.zeros_like(sm)
            sm[0:6, :] = x_refs[0][0:6, :]
            sm[6:7, :] = column_sum(dq_all[...].astype(F32))
            sm[7:8, :] = column_sum(dv_all[...].astype(F32))
            sm[8:12, :] = x_refs[0][8:12, :]
            sm[12:18, :] = x_refs[1][0:6, :]
            sm[18:20, :] = x_refs[2][0:2, :]
            sm[20:24, :] = x_refs[1][8:12, :]
            sm_low[...] = sm[...].astype(BF)
            engine.load(n_early + n_late - 1, lambda part: sm_low)

        if last:
            def complete_rows(i):
                halo = halo_copies()
                at = block_rows(order[i])
                halo[2 * i].wait_recv()
                halo[2 * i + 1].wait_recv()
                low_ref[at, :] = (g_own[at, :] + one[at, :].astype(F32) + two[at, :].astype(F32)).astype(BF)

        def on(t, when, what, *args):
            @pl.when(t == when)
            def _():
                what(*args)

        def begin(copies):
            for copy in copies:
                copy.start()

        def tick(t, carry):
            @pl.when(t < t_back)
            def _():
                one_block(t)

            on(t, t_back, fetch_w.wait)

            @pl.when((t >= t_back) & (t < t_own))
            def _():
                back_rows(t - t_back)

            @pl.when(t == t_own)
            def _():
                begin(halo_copies())
                fetch_r.wait()

            @pl.when((t >= t_own) & (t < t_weight))
            def _():
                own_rows(t - t_own)

            @pl.when(t == t_weight - 1)
            def _():
                begin(fetch_a)

            @pl.when(t == t_weight)
            def _():
                for copy in fetch_a:
                    copy.wait()

            @pl.when((t >= t_weight) & (t < t_rest))
            def _():
                weight_rows(t - t_weight)

            if last:
                @pl.when(t == t_rest)
                def _():
                    late_pieces()

                @pl.when(t == t_rest + 7)
                def _():
                    complete_rows(0)
                    complete_rows(1)
                    deal(True)
                    memory_copies(True)

            busy = t < t_rest

            @pl.when((t % stride == stride - 1) | jnp.logical_not(busy))
            def _():
                engine.round(jnp.where(busy, t // stride, t - t_rest + t_rest // stride))

            return carry

        lax.fori_loop(0, rounds, tick, 0)
        if not last:
            db_out[0:1, :] = column_sum(dq_all[...].astype(F32))
            db_out[1:2, :] = column_sum(dv_all[...].astype(F32))
            db_out[2:8, :] = jnp.zeros((6, width), F32)
            save = pltpu.make_async_copy(dw, dw_out, loc.at[3])
            save.start()
        engine.finish()
        if last:
            for copy in halo_copies():
                copy.wait_send()
        else:
            save.wait()
            for copy in halo_copies():
                copy.wait()
        deal(False)
        memory_copies(False)

    sums_shape = shape_of((engine.n, engine.rows if last else engine.rows // 8, width), BF)
    blocks_shape = shape_of((2, seg, width), BF)
    memory_shape = shape_of((2, 16, width), BF)
    dma = pltpu.SemaphoreType.DMA
    if last:
        out_shape = [
            sums_shape, blocks_shape, memory_shape, shape_of((n_ready, engine.rows, width), BF),
        ]
        out_specs = [ANY, ANY, ANY, ANY]
        more = [
            pltpu.VMEM((own, width), F32),
            pltpu.VMEM((own, width), BF),
            pltpu.VMEM((own, width), BF),
            pltpu.VMEM((size, width), F32),
            pltpu.VMEM((size, width), BF),
        ]
    else:
        out_shape = [
            sums_shape, blocks_shape, memory_shape,
            shape_of((own, width), F32), shape_of((own, width), BF), shape_of((own, width), BF),
            shape_of((3, width, width), BF), shape_of((8, width), F32),
        ]
        out_specs = [WHOLE, ANY, ANY, WHOLE, ANY, ANY, ANY, WHOLE]
        more = []
    return pl.pallas_call(
        kernel,
        out_shape=out_shape,
        in_specs=[ANY, ANY] + [WHOLE] * 7 + [ANY] + [WHOLE] * n_x + [ANY] * n_e + [WHOLE] * int(last),
        out_specs=out_specs,
        scratch_shapes=[
            pltpu.VMEM(w_in.shape, BF),
            pltpu.VMEM((rows, pair_lanes), F32),
            pltpu.VMEM((rows, pair_lanes), F32),
            pltpu.VMEM((rows, width), BF),
            pltpu.VMEM((rows, width), BF),
            pltpu.VMEM((own, width), BF),
            pltpu.VMEM((back, width), BF),
            pltpu.VMEM((3, width, width), BF),
            dma((5,)), dma((5,)), dma((5,)), dma((2,)), dma((2,)),
        ] + more + engine.scratch(),
        compiler_params=pltpu.CompilerParams(
            collective_id=3 if last else 2, has_side_effects=True, vmem_limit_bytes=62 << 20
        ),
        name="attn_bwd_first" if last else "attn_bwd_second",
    )(a, w_in, q, k, v, do, logs, delta, start_row, dr1, *extra, *early, *([ready] if last else []))


def unpack_sums(parts, runs, shard, width):
    size = min(shard, Sums.height)
    starts = [sum(run[2] for run in runs[:i]) for i in range(len(runs))]
    total = sum(run[2] for run in runs)

    def kernel(*refs):
        ins, outs = refs[:len(parts)], refs[len(parts):len(parts) + 4]
        low, high, s_in, s_out = refs[len(parts) + 4:]

        def fetch(start, run, i):
            part, piece, *_ = run
            return pltpu.make_async_copy(
                ins[part].at[piece + i, pl.ds(0, size)], low.at[start + i], s_in.at[start + i]
            )

        def store(start, run, i):
            *_, o, l, tall = run
            rows = pl.ds(pl.multiple_of(i % tall * size, 8), size)
            lanes = pl.ds(pl.multiple_of(i // tall * width, 128), width) if o in (0, 2) else pl.ds(0, width)
            return pltpu.make_async_copy(high.at[start + i], outs[o].at[l, rows, lanes], s_out.at[start + i])

        def for_all(what):
            for start, run in zip(starts, runs):
                def body(i, carry, start=start, run=run):
                    what(start, run, i)
                    return carry

                lax.fori_loop(0, run[2], body, 0)

        def convert(start, run, i):
            fetch(start, run, i).wait()
            high[start + i] = low[start + i].astype(F32)
            store(start, run, i).start()

        for_all(lambda *job: fetch(*job).start())
        for_all(convert)
        for_all(lambda *job: store(*job).wait())

    return pl.pallas_call(
        kernel,
        in_specs=[ANY] * len(parts),
        out_specs=[ANY] * 4,
        out_shape=[
            shape_of((2, shard, 3 * width), F32),
            shape_of((2, shard, width), F32),
            shape_of((2, shard, 4 * width), F32),
            shape_of((2, 4 * shard, width), F32),
        ],
        scratch_shapes=[
            pltpu.VMEM((total, size, width), BF),
            pltpu.VMEM((total, size, width), F32),
            pltpu.SemaphoreType.DMA((total,)),
            pltpu.SemaphoreType.DMA((total,)),
        ],
        compiler_params=pltpu.CompilerParams(vmem_limit_bytes=VMEM_LIMIT),
        name="unpack_sums",
    )(*parts)


def from_behind(x, axis, by):
    length = lax.axis_size(axis)
    pairs = [(i, i + by) for i in range(length) if 0 <= i + by < length]
    return lax.ppermute(x, axis, pairs)


def local(
    hidden_in, read_memory, doc_ids, cotangent, in_weight, in_bias, out_weight, out_bias, gain_one,
    shift_one, up_weight, up_bias, down_weight, down_bias, gain_two, shift_two,
):
    width = hidden_in.shape[-1]
    seg = cotangent.shape[3]
    mem = read_memory.shape[3]
    own = 2 * seg
    back = 2 * own
    heads = width // HEAD_DIM
    contexts = lax.axis_size("ctx")
    fsdps = lax.axis_size("fsdp")
    place = Place(contexts)
    hidden = up_weight.shape[-1]

    documents = doc_ids[0]
    padded = jnp.concatenate([jnp.full((back,), -1, jnp.int32), documents])
    window_doc = lax.dynamic_slice(padded, (place.chunk * own,), (back + own,))
    query_doc = window_doc[back:]
    start = jnp.sum((window_doc[None, :] < query_doc[:, None]).astype(jnp.int32), axis=1)
    start_col, start_row = start[:, None], start[None, :]

    vectors = [out_bias, gain_one, shift_one, down_bias, gain_two, shift_two]
    six = jnp.stack(vectors, axis=1)
    part = width // fsdps
    packed = jnp.concatenate(
        [six.reshape(2, 6 * part), in_bias, up_bias], axis=1
    ).reshape(-1, 128)

    x0 = jnp.concatenate([read_memory[0, 0], hidden_in[0, 0]], axis=1)
    weights = (in_weight, out_weight, up_weight, down_weight)
    a1, in_1, out_1, up_1, down_1, packed_all = fetch_window(x0, weights, packed, contexts, fsdps, 0)

    packed_all = packed_all.reshape(fsdps, 2, 12 * part).astype(F32)
    six_all = packed_all[:, :, :6 * part].reshape(fsdps, 2, 6, part).transpose(1, 2, 0, 3).reshape(2, 6, 1, width)
    qv_bias = packed_all[:, :, 6 * part:8 * part].transpose(1, 0, 2).reshape(2, 1, 2 * width)
    up_all = packed_all[:, :, 8 * part:].transpose(1, 0, 2).reshape(2, 1, hidden)

    pick_rows = lax.broadcasted_iota(jnp.int32, (heads // 4 * 8, width), 0)
    pick_lane = lax.broadcasted_iota(jnp.int32, (heads // 4 * 8, width), 1) // HEAD_DIM
    pick = ((pick_lane // 4 == pick_rows // 8) & (pick_lane % 4 == pick_rows % 8)).astype(BF)

    def forward(a, h, h_block, w, l):
        w_in, w_out, w_up, w_down = w
        bo, g1, s1, bd, g2, s2 = (six_all[l, i] for i in range(6))
        q, k, v, att, logs = attn_fwd(a, w_in, qv_bias[l], start_col, seg)
        xh1, rs1, mid_low, act, gp, xh2, rs2, out, out_low = ff_fwd(
            att, h, h_block, w_out, w_up, w_down, bo, up_all[l], bd, g1, s1, g2, s2
        )
        return out, out_low, (a, w, l, q, k, v, att, logs, xh1, rs1, mid_low, act, gp, xh2, rs2)

    def backward(grads, saved):
        a, (w_in, w_out, w_up, w_down), l, q, k, v, att, logs, xh1, rs1, mid_low, act, gp, xh2, rs2 = saved
        g1, g2 = six_all[l, 1], six_all[l, 4]
        dwd, dwu, dwo, small, dr1, do, delta = ff_bwd(
            grads, xh2, rs2, g2, gp, act, w_down, w_up, mid_low, xh1, rs1, g1, w_out, att, pick
        )
        delta = delta.reshape(heads // 4, 8, own)
        return small, [dwd, dwu, dwo], (a, w_in, q, k, v, do, logs, delta, start_row, dr1, seg, contexts, fsdps)

    h1, h1_low, saved_1 = forward(a1, a1, 2, (in_1, out_1, up_1, down_1), 0)
    a2, in_2, out_2, up_2, down_2, cot = share_window(h1_low, weights, cotangent[0, 0], contexts, fsdps, 1)
    _, h2_low, saved_2 = forward(a2, h1, 0, (in_2, out_2, up_2, down_2), 1)

    small_2, early_2, state = backward([cot], saved_2)
    scattered, activations, write, g_own, from_one, from_two, dw_2, db_2 = attn_bwd(*state, early_2, (h2_low,))
    small_1, early_1, state = backward([g_own, from_one, from_two], saved_1)
    sums_1, dealt, reads, sums_2 = attn_bwd(
        *state, [dw_2] + early_1, (small_1, small_2, db_2), scattered
    )

    write = write[:, 16 - mem:]
    first = jnp.where(place.me == 0, read_memory[0, 0, 0], write[0])
    new_memory = jnp.stack([first, write[1]])[None, None]
    input_grad = dealt[:, mem:][None, None]
    reads = reads[:, :mem]
    second = jnp.where(place.me == 0, jnp.zeros_like(reads[1]), reads[1])
    memory_grad = jnp.stack([reads[0], second])[None, None]

    shard = width // fsdps

    tall = shard // min(shard, Sums.height)

    def ff_runs(part, first, l):
        return [
            (part, first, 4 * tall, 3, l, 4 * tall),
            (part, first + 4 * tall, 4 * tall, 2, l, tall),
            (part, first + 8 * tall, tall, 1, l, tall),
        ]

    runs = ff_runs(0, 0, 1) + [(1, 0, 3 * tall, 0, 1, tall)] + ff_runs(1, 3 * tall, 0)
    runs.append((1, 12 * tall, 3 * tall, 0, 0, tall))
    in_grad, out_grad, up_grad, down_grad = unpack_sums([sums_2, sums_1], runs, shard, width)

    rows = sums_1[-1, :24].astype(F32).reshape(2, 12, width)
    f = place.f

    def own_part(x):
        size = x.shape[-1] // fsdps
        return lax.dynamic_slice(x, (0, f * size), (2, size))

    dg2, ds2, dbd, dg1, ds1, dbo = (own_part(rows[:, i]) for i in range(6))
    d_in_bias = own_part(rows[:, 6:8].reshape(2, 2 * width))
    d_up_bias = own_part(rows[:, 8:12].reshape(2, hidden))
    return (
        activations[None, None], new_memory, input_grad, memory_grad, in_grad, d_in_bias, out_grad, dbo,
        dg1, ds1, up_grad, d_up_bias, down_grad, dbd, dg2, ds2,
    )


def solution(mesh):
    row = P("fsdp", "ctx", None, None, None)
    mat = P(None, "fsdp", None)
    vec = P(None, "fsdp")
    params = (mat, vec, mat, vec, vec, vec, mat, vec, mat, vec, vec, vec)
    return jax.shard_map(
        local,
        mesh=mesh,
        in_specs=(row, row, P("fsdp", None), row) + params,
        out_specs=(row, row, row, row) + params,
        check_vma=False,
    )
```
